128 devices in a mesh: row: 8 (over y_hi, z), col: 16 (over x, y_lo, core).
Axes of the slice: x: 4, y: 4 (y_hi: 2, y_lo: 2; y = y_hi * 2 + y_lo), z: 4, core: 2. Of those that a mesh axis runs over, the one named last changes fastest.
Arguments:
- a_vals: bfloat16 [128, 32, 128, 128], P('row', 'col'), may hold values from -0.21875 to 0.21875
- a_cols: int32 [128, 32], P('row', 'col'), may hold values from 0 to 127, as said below
- b_vals: bfloat16 [128, 48, 128, 128], P('row', 'col'), may hold values from -6 to 6
- b_cols: int32 [128, 48], P('row', 'col'), may hold values from 0 to 255, as said below
- c_cols: int32 [128, 128], P('row', 'col'), may hold values from 0 to 255, as said below
- c_send: int32 [8, 16, 128], P('row', 'col'), may hold values from 0 to 127, each once within a row
Outputs:
- c_owned: bfloat16 [16384, 128, 128], P(('row', 'col'))
The draws below stay inside these ranges and needn't reach their ends.
Inputs may be any that keep to these rules, and one draw needn't show every extreme that they name: `a_cols`: the entries of block row i in slot group c are 2 distinct block columns of panel c, c * 8 to (c + 1) * 8 - 1. `b_cols`: the entries of block row k in slot group c are 3 distinct block columns c * 16 to (c + 1) * 16 - 1. `c_cols`: the entries of block row i in slot group c are 8 distinct block columns c * 16 to (c + 1) * 16 - 1.
All inputs are finite; a program needn't handle non-finite values.
Results may differ from the reference program's by a relative error of at most 0.001.
Values may be sent and summed in bfloat16 or wider, within the bound.
A program may use at most 384 MiB of HBM per device.

```python
import jax
import jax.numpy as jnp
from jax import lax

BS = 128
SBD = 16
NZS = 2
NZBC = 3
NZC = 8
RB_DEV = 16
MB = 128
KB = 128
PANEL = 8
SB = 256
KEPT = 128
PER = 1
C_BLOCKS = 16384
N_ROW = 8
N_COL = 16


def distinct_lists(key, row_count, group_count, per_group, span_len):
    subkeys = jax.random.split(key, row_count * group_count)
    chosen = jax.vmap(lambda item_key: jax.random.permutation(item_key, span_len)[:per_group])(subkeys)
    chosen = chosen.reshape(row_count, group_count, per_group).astype(jnp.int32)
    anchor = (jnp.arange(group_count, dtype=jnp.int32) * span_len)[None, :, None]
    return (chosen + anchor).reshape(row_count, group_count * per_group)


def draw_a_cols(key, part):
    return distinct_lists(jax.random.fold_in(key, 11), MB, KB // PANEL, NZS, PANEL)


def draw_b_cols(key, part):
    return distinct_lists(jax.random.fold_in(key, 23), KB, SB // SBD, NZBC, SBD)


def draw_c_cols(key, part):
    return distinct_lists(jax.random.fold_in(key, 37), MB, SB // SBD, NZC, SBD)


def shard_levels(rng, extent, cuts, low, top_value):
    def one(dim, shards_of):
        draws = jax.random.uniform(jax.random.fold_in(jax.random.fold_in(rng, 6), dim), (shards_of,), jnp.float32, low / len(cuts), top_value / len(cuts))
        return jnp.repeat(jnp.exp(draws), extent[dim] // shards_of).reshape((-1,) + (1,) * (len(extent) - dim - 1))

    factor_of = one(*cuts[0])
    for cut in cuts[1:]:
        factor_of = factor_of * one(*cut)
    return factor_of


def noise(own_key, shape, spread, reach, cuts=(), kind=jnp.bfloat16):
    result = spread * jax.random.normal(own_key, shape, jnp.float32)
    if cuts:
        result = result * shard_levels(own_key, shape, cuts, -0.22, 0.18)
    return jnp.clip(result, -reach, reach).astype(kind)


def setup_inputs(seed: int = 0) -> dict:
    key_of = jax.random.split(jax.random.key(seed), 7)
    return {
        "a_vals": noise(key_of[0], (MB, N_COL * NZS, BS, BS), (BS * N_COL * NZS * NZBC // SBD) ** -0.5, 0.21875, ((0, 8), (1, 16))),
        "a_cols": draw_a_cols(jax.random.fold_in(key_of[6], 71), 0),
        "b_vals": noise(key_of[2], (KB, N_COL * NZBC, BS, BS), 1.0, 6.0, ((0, 8), (1, 16))),
        "b_cols": draw_b_cols(jax.random.fold_in(key_of[6], 71), 0),
        "c_cols": draw_c_cols(jax.random.fold_in(key_of[6], 71), 0),
        "c_send": jax.vmap(lambda own: jax.random.permutation(own, KEPT))(jax.random.split(key_of[5], N_ROW * N_COL)).reshape((N_ROW, N_COL, KEPT)).astype(jnp.int32),
    }


def reference(a_vals, a_cols, b_vals, b_cols, c_cols, c_send):
    groups = N_COL

    def one_row(inputs):
        a_row, k_row, keep_row = inputs
        slot_count = k_row.shape[0]
        b_rows = jnp.take(b_vals, k_row, axis=0).astype(jnp.float32)
        b_rows = b_rows.reshape(slot_count, groups, NZBC, BS, BS)
        col_rows = jnp.take(b_cols, k_row, axis=0).reshape(slot_count, groups, NZBC)
        products = jnp.einsum('sab,scqbd->scqad', a_row.astype(jnp.float32), b_rows, precision=lax.Precision.HIGHEST)
        keep_grid = keep_row.reshape(groups, NZC)
        matches = (col_rows[:, :, :, None] == keep_grid[None, :, None, :]).astype(jnp.float32)
        kept_rows = jnp.einsum('scqn,scqad->cnad', matches, products, precision=lax.Precision.HIGHEST)
        return kept_rows.astype(jnp.bfloat16)

    kept_all = lax.map(one_row, (a_vals, a_cols, c_cols))
    device_count = N_ROW * N_COL
    kept_dev = kept_all.reshape(N_ROW, RB_DEV, N_COL, NZC, BS, BS)
    kept_dev = kept_dev.transpose(0, 2, 1, 3, 4, 5).reshape(device_count, KEPT, BS, BS)
    send_order = c_send.reshape(device_count, KEPT).astype(jnp.int32)
    outgoing = jnp.take_along_axis(kept_dev, send_order[:, :, None, None], axis=1)
    owned = outgoing.reshape(device_count, device_count, PER, BS, BS).transpose(1, 0, 2, 3, 4)
    return owned.reshape(C_BLOCKS, BS, BS)
```

```python
import jax
import jax.numpy as jnp
from jax import lax
from jax.experimental import pallas as pl
from jax.experimental.pallas import tpu as pltpu
from jax.sharding import PartitionSpec as P

MESH = pl.DeviceIdType.MESH
N_ROW, N_COL = 8, 16
NX, NZ = 4, 4
BS = 128
SBD, PANEL = 16, 8
RB, NZS, NZBC, NZC = 16, 2, 3, 8
KEPT = RB * NZC
SLOTS = N_COL * NZS
ZERO = N_ROW * RB * NZBC
LIST_ROWS = SLOTS + 8
CODE = 512
HALF = RB // 2


def build_lists(aidx, bidx, ccol_ref, arep, brep, list_ref):
    for c in range(N_COL):
        arep[pl.ds(c, 1), :] = aidx[c, 2:3, :]
    for r in range(N_ROW):
        brep[pl.ds(2 * r, 2), :] = bidx[r, 0:2, :]
    lane_in = lax.broadcasted_iota(jnp.int32, (BS, BS), 0)
    lane_out = lax.broadcasted_iota(jnp.int32, (BS, BS), 1)
    offs = arep[...].astype(jnp.bfloat16)
    spread = []
    for s in range(NZS):
        pick = (lane_in == NZS * (lane_out // NZC) + s).astype(jnp.bfloat16)
        spread.append(jnp.dot(offs, pick, preferred_element_type=jnp.float32))
    aoff = jnp.concatenate(spread, axis=0).astype(jnp.int32)
    cols = jnp.concatenate([brep[...], brep[...]], axis=0)
    keep = jnp.broadcast_to(ccol_ref[0:1, :], (SLOTS, KEPT))
    turn = lax.broadcasted_iota(jnp.int32, (SLOTS, KEPT), 0)
    panel = turn % N_COL
    which = turn // N_COL
    found = jnp.zeros((SLOTS, KEPT), jnp.int32)
    for j in range(PANEL):
        here = aoff == j
        for q in range(NZBC):
            at = NZBC * j + q
            col = jnp.broadcast_to(cols[:, at : at + 1], (SLOTS, KEPT))
            found = jnp.where(here & (col == keep), panel * (PANEL * NZBC) + at + 1, found)
    hit = found > 0
    hits = hit.astype(jnp.float32).astype(jnp.bfloat16)
    row_id = lax.broadcasted_iota(jnp.int32, (SLOTS, SLOTS), 0)
    col_id = lax.broadcasted_iota(jnp.int32, (SLOTS, SLOTS), 1)
    below = (col_id < row_id).astype(jnp.float32).astype(jnp.bfloat16)
    rank = jnp.dot(below, hits, preferred_element_type=jnp.float32).astype(jnp.int32)
    rank = jnp.where(hit, rank, SLOTS)
    count = jnp.sum(hit.astype(jnp.int32), axis=0, keepdims=True)
    full = (panel * NZS + which) * CODE + found - 1
    for n in range(SLOTS):
        entry = jnp.sum(jnp.where(rank == n, full, 0), axis=0, keepdims=True)
        list_ref[pl.ds(n, 1), :] = jnp.where(count > n, entry, ZERO)
    list_ref[pl.ds(SLOTS, 8), :] = jnp.broadcast_to(count, (8, KEPT))


def gather_kernel(
    idx_ref, ccol_ref, a_ref, b_ref, a_all, b_all, list_ref,
    aidx, bidx, arep, brep, a_own, b_own, send, recv, isend, irecv, lsem,
):
    row, col = lax.axis_index("row"), lax.axis_index("col")
    yh, z = row // NZ, row % NZ
    x, yl, core = col // 4, (col // 2) % 2, col % 2

    def at_z(h, zz):
        return lax.rem(yh + h, 2) * NZ + lax.rem(zz + NZ, NZ)

    def at_x(h, xx):
        return lax.rem(xx + NX, NX) * 4 + lax.rem(yl + h, 2) * 2 + core

    twin = (row, col + 1 - 2 * core)
    barrier = pltpu.get_barrier_semaphore()
    row_peers = [(lax.rem(row + j, N_ROW), col) for j in range(1, N_ROW)]
    col_peers = [(row, lax.rem(col + j, N_COL)) for j in range(1, N_COL)]
    for peer in row_peers + col_peers:
        pl.semaphore_signal(barrier, inc=1, device_id=peer, device_id_type=MESH)
    pl.semaphore_wait(barrier, len(row_peers) + len(col_peers))

    started = []

    def put(src, dst, peer):
        n = len(started)
        copy = pltpu.make_async_remote_copy(
            src_ref=src, dst_ref=dst, send_sem=send.at[n], recv_sem=recv.at[n],
            device_id=peer, device_id_type=MESH,
        )
        copy.start()
        started.append(copy)
        return copy

    def piece(ref, slot, half):
        return ref.at[slot, pl.ds(half * HALF, HALF)]

    def b_src(h, half):
        return b_ref.at[pl.ds(half * HALF, HALF)] if h == 0 else piece(b_all, at_z(1, z), half)

    def a_src(h, half):
        return a_ref.at[pl.ds(half * HALF, HALF)] if h == 0 else piece(a_all, at_x(1, x), half)

    up, down = (at_z(0, z + 1), col), (at_z(0, z - 1), col)
    east, west = (row, at_x(0, x + 1)), (row, at_x(0, x - 1))

    def ring(src, whole, at, pos, h, plus, minus):
        slot = at(h, pos)
        p0 = put(src(h, 0), piece(whole, slot, 0), plus)
        m1 = put(src(h, 1), piece(whole, slot, 1), minus)
        p1 = put(src(h, 1), piece(whole, slot, 1), plus)
        m0 = put(src(h, 0), piece(whole, slot, 0), minus)
        return p0, m1, p1, m0

    def pass_on(whole, at, pos, h, step, half, peer):
        part = piece(whole, at(h, pos + step), half)
        return put(part, part, peer)

    def a_hand(h, step, half):
        part = piece(a_all, at_x(h, x + step), half)
        return put(part, part, twin)

    small = []
    for n, peer in enumerate(row_peers):
        copy = pltpu.make_async_remote_copy(
            src_ref=idx_ref, dst_ref=bidx.at[row], send_sem=isend.at[n], recv_sem=irecv.at[n],
            device_id=peer, device_id_type=MESH,
        )
        copy.start()
        small.append(copy)
    for n, peer in enumerate(col_peers):
        n = n + len(row_peers)
        copy = pltpu.make_async_remote_copy(
            src_ref=idx_ref, dst_ref=aidx.at[col], send_sem=isend.at[n], recv_sem=irecv.at[n],
            device_id=peer, device_id_type=MESH,
        )
        copy.start()
        small.append(copy)

    a_across = put(a_ref, a_all.at[col], (row, at_x(1, x)))
    b0 = ring(b_src, b_all, at_z, z, 0, up, down)
    a0 = ring(a_src, a_all, at_x, x, 0, east, west)
    b_across = put(b_ref, b_all.at[row], (at_z(1, z), col))
    handed = [put(a_ref, a_all.at[col], twin)]

    b_in = pltpu.make_async_copy(b_ref, b_own, lsem.at[0])
    a_in = pltpu.make_async_copy(a_ref, a_own, lsem.at[1])
    b_in.start()
    a_in.start()
    b_in.wait()
    b_out = pltpu.make_async_copy(b_own, b_all.at[row], lsem.at[2])
    b_out.start()
    a_in.wait()
    a_out = pltpu.make_async_copy(a_own, a_all.at[col], lsem.at[3])
    a_out.start()

    aidx[col] = idx_ref[...]
    bidx[row] = idx_ref[...]
    for copy in small:
        copy.wait_recv()
    build_lists(aidx, bidx, ccol_ref, arep, brep, list_ref)

    def first_hop_near(ring_copies, whole, at, pos, h, plus, minus):
        p0, m1, _, _ = ring_copies
        p0.wait_recv()
        f0 = pass_on(whole, at, pos, h, -1, 0, plus)
        m1.wait_recv()
        f1 = pass_on(whole, at, pos, h, 1, 1, minus)
        return f0, f1

    a0f = first_hop_near(a0, a_all, at_x, x, 0, east, west)
    handed += [a_hand(0, -1, 0), a_hand(0, 1, 1)]
    b0f = first_hop_near(b0, b_all, at_z, z, 0, up, down)
    a0[2].wait_recv()
    a0[3].wait_recv()
    handed += [a_hand(0, -1, 1), a_hand(0, 1, 0)]
    a_across.wait_recv()
    a1 = ring(a_src, a_all, at_x, x, 1, east, west)
    handed += [put(a_all.at[at_x(1, x)], a_all.at[at_x(1, x)], twin)]
    b0[2].wait_recv()
    b0[3].wait_recv()
    b_across.wait_recv()
    b1 = ring(b_src, b_all, at_z, z, 1, up, down)
    a0f[0].wait_recv()
    a0f[1].wait_recv()
    handed += [a_hand(0, 2, 0), a_hand(0, 2, 1)]
    a1f = first_hop_near(a1, a_all, at_x, x, 1, east, west)
    handed += [a_hand(1, -1, 0), a_hand(1, 1, 1)]
    a1[2].wait_recv()
    a1[3].wait_recv()
    handed += [a_hand(1, -1, 1), a_hand(1, 1, 0)]
    b0f[0].wait_recv()
    b0f[1].wait_recv()
    b1f = first_hop_near(b1, b_all, at_z, z, 1, up, down)
    a1f[0].wait_recv()
    a1f[1].wait_recv()
    handed += [a_hand(1, 2, 0), a_hand(1, 2, 1)]
    b1[2].wait_recv()
    b1[3].wait_recv()
    b1f[0].wait_recv()
    b1f[1].wait_recv()
    for copy in handed:
        copy.wait_recv()
    for copy in small + started:
        copy.wait_send()
    b_out.wait()
    a_out.wait()


N_COPIES = 41


def gather(idx, keep, a_vals, b_vals):
    any_space = pl.BlockSpec(memory_space=pl.ANY)
    vmem = pl.BlockSpec(memory_space=pltpu.VMEM)
    return pl.pallas_call(
        gather_kernel,
        name="gather",
        out_shape=(
            jax.ShapeDtypeStruct((N_COL, RB, NZS, BS, BS), jnp.bfloat16),
            jax.ShapeDtypeStruct((N_ROW, RB, NZBC, BS, BS), jnp.bfloat16),
            jax.ShapeDtypeStruct((LIST_ROWS, KEPT), jnp.int32),
        ),
        in_specs=[vmem, vmem, any_space, any_space],
        out_specs=(any_space, any_space, vmem),
        scratch_shapes=[
            pltpu.VMEM((N_COL, 8, 128), jnp.int32),
            pltpu.VMEM((N_ROW, 8, 128), jnp.int32),
            pltpu.VMEM((N_COL, 128), jnp.int32),
            pltpu.VMEM((N_COL, 128), jnp.int32),
            pltpu.VMEM((RB, NZS, BS, BS), jnp.bfloat16),
            pltpu.VMEM((RB, NZBC, BS, BS), jnp.bfloat16),
            pltpu.SemaphoreType.DMA((N_COPIES,)),
            pltpu.SemaphoreType.DMA((N_COPIES,)),
            pltpu.SemaphoreType.DMA((N_ROW + N_COL - 2,)),
            pltpu.SemaphoreType.DMA((N_ROW + N_COL - 2,)),
            pltpu.SemaphoreType.DMA((4,)),
        ],
        compiler_params=pltpu.CompilerParams(collective_id=0, has_side_effects=True),
    )(idx, keep, a_vals, b_vals)


def product_kernel(
    list_ref, order_ref, a_all, b_all, out_ref, a_buf, b_buf, acc, kept, place, a_sem, b_sem, o_sem
):
    def a_copy(i, slot):
        return pltpu.make_async_copy(
            a_all.at[:, i], a_buf.at[slot], a_sem.at[slot]
        )

    b_copy = pltpu.make_async_copy(b_all, b_buf.at[pl.ds(0, ZERO)], b_sem)
    a_copy(0, 0).start()
    b_copy.start()
    b_buf[ZERO] = jnp.zeros((BS, BS), jnp.bfloat16)

    @pl.loop(0, KEPT)
    def _(d):
        place[order_ref[d]] = d

    b_copy.wait()

    @pl.loop(0, RB)
    def _(i):
        slot = i % 2

        @pl.when(i + 1 < RB)
        def _():
            a_copy(i + 1, 1 - slot).start()

        a_copy(i, slot).wait()
        most = list_ref[SLOTS, i * NZC]
        for m in range(1, NZC):
            most = jnp.maximum(most, list_ref[SLOTS, i * NZC + m])
        acc[...] = jnp.zeros_like(acc)

        @pl.loop(0, (most + 1) // 2)
        def _(t):
            for m in range(NZC):
                one = list_ref[2 * t, i * NZC + m]
                two = list_ref[2 * t + 1, i * NZC + m]
                p1, p2 = one // CODE, two // CODE
                left = jnp.concatenate(
                    [a_buf[slot, p1 // NZS, p1 % NZS], a_buf[slot, p2 // NZS, p2 % NZS]], axis=1
                )
                right = jnp.concatenate([b_buf[one % CODE], b_buf[two % CODE]], axis=0)
                acc[m] += jnp.dot(left, right, preferred_element_type=jnp.float32)

        for m in range(NZC):
            o = i * NZC + m
            kept[o] = acc[m].astype(jnp.bfloat16)
            pltpu.make_async_copy(kept.at[o], out_ref.at[place[o]], o_sem).start()

    pltpu.make_async_copy(kept, out_ref, o_sem).wait()


def product(lists, order, a_all, b_all):
    any_space = pl.BlockSpec(memory_space=pl.ANY)
    smem = pl.BlockSpec(memory_space=pltpu.SMEM)
    b_all = b_all.reshape(ZERO, BS, BS)
    return pl.pallas_call(
        product_kernel,
        name="product",
        out_shape=jax.ShapeDtypeStruct((KEPT, BS, BS), jnp.bfloat16),
        in_specs=[smem, smem, any_space, any_space],
        out_specs=any_space,
        scratch_shapes=[
            pltpu.VMEM((2, N_COL, NZS, BS, BS), jnp.bfloat16),
            pltpu.VMEM((ZERO + 1, BS, BS), jnp.bfloat16),
            pltpu.VMEM((NZC, BS, BS), jnp.float32),
            pltpu.VMEM((KEPT, BS, BS), jnp.bfloat16),
            pltpu.SMEM((KEPT,), jnp.int32),
            pltpu.SemaphoreType.DMA((2,)),
            pltpu.SemaphoreType.DMA,
            pltpu.SemaphoreType.DMA,
        ],
    )(lists, order, a_all, b_all)


def on_device(a_vals, a_cols, b_vals, b_cols, c_cols, c_send):
    col = lax.axis_index("col")
    wide = lambda part: jnp.pad(part, ((0, 0), (0, 128 - part.shape[1])))
    b_local = (b_cols - col * SBD).reshape(2, PANEL * NZBC)
    a_local = (a_cols - col * PANEL).reshape(1, RB * NZS)
    idx = jnp.concatenate([wide(b_local), wide(a_local), jnp.zeros((5, 128), jnp.int32)], axis=0)
    keep = (c_cols - col * SBD).reshape(1, KEPT)
    a_all, b_all, lists = gather(idx, keep, a_vals, b_vals)
    outgoing = product(lists, c_send.reshape(KEPT), a_all, b_all)
    return lax.all_to_all(outgoing, ("row", "col"), split_axis=0, concat_axis=0, tiled=True)


def solution(mesh):
    in_specs = (
        P("row", "col", None, None),
        P("row", "col"),
        P("row", "col", None, None),
        P("row", "col"),
        P("row", "col"),
        P("row", "col", None),
    )
    out_specs = P(("row", "col"), None, None)
    return jax.shard_map(
        on_device, mesh=mesh, in_specs=in_specs, out_specs=out_specs, check_vma=False
    )
```
